256 devices in a mesh: mem: 16 (over y, x_hi, core), lat: 16 (over z, x_lo).
Axes of the slice: x: 4 (x_hi: 2, x_lo: 2; x = x_hi * 2 + x_lo), y: 4, z: 8, core: 2. Of those that a mesh axis runs over, the one named last changes fastest.
Arguments:
- members: bfloat16 [80, 2, 4, 128, 1152], P('mem', None, None, 'lat'), may hold values from -0.625 to 0.625
- alpha: float32 [80, 4, 128, 1152], P('mem', None, 'lat'), may hold values from -6 to 6
- zonal_loc: bfloat16 [1152, 1152], replicated
- merid_coef: float32 [128, 9], replicated, may hold values from 0.1 to 0.6
- slot_tile: int32 [16, 16, 3], P('lat', 'mem'), may hold values from 0 to 17, as said below
- obs_count: int32 [16, 16, 3], P('lat', 'mem'), may hold values from 0 to 4096, as said below
- obs_index: int32 [16, 16, 3, 4096], P('lat', 'mem'), may hold values from 0 to 16383
- obs_value: float32 [16, 16, 3, 4096], P('lat', 'mem'), may hold values from -6 to 6
- obs_weight: float32 [16, 16, 3, 4096], P('lat', 'mem'), may hold values from 0.5 to 4
Outputs:
- analysis_alpha: float32 [80, 4, 128, 1152], P('mem', None, 'lat')
The draws below stay inside these ranges and needn't reach their ends.
Inputs may be any that keep to these rules, and one draw needn't show every extreme that they name: `slot_tile`: within each band every tile 0..17 stands in exactly one slot; a device owns at most 3 tiles of a band, and in every band one device owns exactly 3. Unused slots hold tile 0. `obs_count`: zero exactly in unused slots; a used slot holds 4096, 2048 or 1024 live observations, and each band has a slot with 4096.
All inputs are finite; a program needn't handle non-finite values.
Results may differ from the reference program's by a relative error of at most 0.00065.
Values may be sent and summed in bfloat16 or wider, within the bound.
A program may use at most 64 MiB of HBM per device.

```python
import math
import jax
import jax.numpy as jnp
from jax import lax

MEMBERS = 80
VARS = 2
LEV = 4
NLON = 1152
CLAT_DEV = 8
BAND = 4
TLON = 128
MAXOWN = 3
OBS_TILE = 4096
ITERS = 2
BANDS = 16
CLAT = 128
NTILE = 18
TILE_CELLS = 16384
N_MEM = 16


def draw_zonal_loc(key, part):
    columns = jnp.arange(NLON)
    distance = jnp.abs(columns[:, None] - columns[None, :])
    distance = jnp.minimum(distance, NLON - distance).astype(jnp.float32)
    length_scale = NLON / 4.0
    roughness = jax.random.uniform(key, (NLON, NLON), jnp.float32, 0.4, 1.6)
    off_diag = 0.035 * jnp.exp(-0.5 * (distance / length_scale) ** 2) * roughness
    return jnp.where(distance == 0, jnp.float32(1.0), off_diag).astype(jnp.bfloat16)


def ownership_band(band_key):
    tile_key, device_key, count_key = jax.random.split(band_key, 3)
    tile_perm = jax.random.permutation(tile_key, NTILE).astype(jnp.int32)
    device_perm = jax.random.permutation(device_key, N_MEM).astype(jnp.int32)
    position = jnp.arange(NTILE, dtype=jnp.int32)
    remainder = jnp.maximum(position - MAXOWN, 0)
    others = N_MEM - 1
    device = jnp.where(position < MAXOWN, device_perm[0], device_perm[1 + remainder % others])
    slot_place = jnp.where(position < MAXOWN, position, remainder // others)
    halvings = jax.random.randint(count_key, (NTILE,), 0, 3)
    live_counts = OBS_TILE // jnp.left_shift(jnp.int32(1), halvings.astype(jnp.int32))
    live_counts = jnp.where(position == 0, OBS_TILE, live_counts).astype(jnp.int32)
    tile_table = jnp.zeros((N_MEM, MAXOWN), jnp.int32).at[device, slot_place].set(tile_perm)
    count_table = jnp.zeros((N_MEM, MAXOWN), jnp.int32).at[device, slot_place].set(live_counts)
    return (tile_table, count_table)


def ownership(key):
    base_key = jax.random.fold_in(key, 7)
    band_keys = jax.random.split(base_key, BANDS)
    return jax.vmap(ownership_band)(band_keys)


def draw_slot_tile(key, part):
    return ownership(key)[0]


def draw_obs_count(key, part):
    return ownership(key)[1]


def place_ends(array, own_key, low, largest):
    longest = array.shape.index(max(array.shape))
    spots = []
    for shift in (0, 1):
        where = [jax.random.randint(jax.random.fold_in(own_key, axis), (), 0, length) for axis, length in enumerate(array.shape)]
        where[longest] = (where[longest] + shift) % array.shape[longest]
        spots.append(tuple(where))
    return array.at[spots[0]].set(low).at[spots[1]].set(largest)


def level_of(stream_key, shape, pieces, low, high):
    factor_of = 1.0
    for axis_at, blocks in pieces:
        steps = jax.random.uniform(jax.random.fold_in(jax.random.fold_in(stream_key, 6), axis_at), (blocks,), jnp.float32, low / len(pieces), high / len(pieces))
        factor_of = factor_of * jnp.repeat(jnp.exp(steps), shape[axis_at] // blocks).reshape((-1,) + (1,) * (len(shape) - 1 - axis_at))
    return factor_of


def scatter_about(stream_key, extent, scale, reach, cuts=(), kind=jnp.bfloat16):
    loudness = level_of(stream_key, extent, cuts, -0.22, 0.18) if cuts else 1.0
    array = jax.random.normal(stream_key, extent, jnp.float32) * scale * loudness
    return jnp.minimum(jnp.maximum(array, -reach), reach).astype(kind)


def setup_inputs(seed: int = 0) -> dict:
    splits = jax.random.split(jax.random.key(seed), 10)
    members = scatter_about(splits[0], (MEMBERS, VARS, LEV, CLAT, NLON), MEMBERS ** -0.5, 0.625, ((0, 16), (3, 16)))
    alpha = scatter_about(splits[1], (MEMBERS, LEV, CLAT, NLON), 1.0, 6.0, ((0, 16), (2, 16)), jnp.float32)
    zonal_loc = draw_zonal_loc(jax.random.fold_in(splits[9], 71), 0)
    merid_coef = jnp.clip(jax.random.uniform(splits[3], (CLAT, 2 * BAND + 1), jnp.float32, 0.1, 0.6), 0.1, 0.6)
    slot_tile = draw_slot_tile(jax.random.fold_in(splits[9], 71), 0)
    obs_count = draw_obs_count(jax.random.fold_in(splits[9], 71), 0)
    obs_index = place_ends(jax.random.randint(splits[6], (BANDS, N_MEM, MAXOWN, OBS_TILE), 0, TILE_CELLS), jax.random.fold_in(splits[6], 1), 0, TILE_CELLS - 1).astype(jnp.int32)
    obs_value = scatter_about(splits[7], (BANDS, N_MEM, MAXOWN, OBS_TILE), 1.0, 6.0, ((0, 16), (1, 16)), jnp.float32)
    obs_weight = jnp.clip(jnp.exp(math.log(4.0) - 2.0794415 * jax.random.uniform(splits[8], (BANDS, N_MEM, MAXOWN, OBS_TILE), jnp.float32) ** level_of(splits[8], (BANDS, N_MEM, MAXOWN, OBS_TILE), ((0, 16), (1, 16)), -0.2, 0.2)), 0.5, 4.0)
    return dict(members=members, alpha=alpha, zonal_loc=zonal_loc, merid_coef=merid_coef, slot_tile=slot_tile, obs_count=obs_count, obs_index=obs_index, obs_value=obs_value, obs_weight=obs_weight)


step_size = 0.3

def localize(member_alpha, merid_coef, zonal_loc):
    alpha_pad = jnp.pad(member_alpha, ((0, 0), (BAND, BAND), (0, 0)))
    running = jnp.zeros(member_alpha.shape, jnp.float32)
    for offset in range(-BAND, BAND + 1):
        running = running + merid_coef[:, offset + BAND][None, :, None] * alpha_pad[:, BAND + offset:BAND + offset + CLAT]
    spread = running.astype(jnp.bfloat16)
    zonal_out = jnp.dot(spread.reshape(-1, NLON), zonal_loc, preferred_element_type=jnp.float32)
    return zonal_out.reshape(member_alpha.shape)

def meridional_back(zonal_back, merid_coef):
    back_pad = jnp.pad(zonal_back, ((0, 0), (BAND, BAND), (0, 0)))
    coef_pad = jnp.pad(merid_coef, ((BAND, BAND), (0, 0)))
    running = jnp.zeros(zonal_back.shape, jnp.float32)
    for offset in range(-BAND, BAND + 1):
        running = running + coef_pad[BAND - offset:BAND - offset + CLAT, offset + BAND][None, :, None] * back_pad[:, BAND - offset:BAND - offset + CLAT]
    return running

def interpolate(increment):
    padded = jnp.concatenate([increment[:, :, :1], increment, increment[:, :, -1:]], axis=2)
    even_rows = 0.75 * padded[:, :, 1:-1] + 0.25 * padded[:, :, :-2]
    odd_rows = 0.75 * padded[:, :, 1:-1] + 0.25 * padded[:, :, 2:]
    merid = jnp.stack([even_rows, odd_rows], axis=3).reshape(VARS, LEV, 2 * CLAT, NLON)
    shifted = jnp.roll(merid, -1, axis=3)
    return jnp.stack([merid, 0.5 * (merid + shifted)], axis=-1).reshape(VARS, LEV, 2 * CLAT, 2 * NLON)

def to_tiles(fine_field):
    shaped = fine_field.reshape(VARS, LEV, BANDS, 2 * CLAT_DEV, NTILE, TLON)
    return shaped.transpose(2, 4, 0, 1, 3, 5).reshape(-1)

def from_tiles(flat_tiles):
    shaped = flat_tiles.reshape(BANDS, NTILE, VARS, LEV, 2 * CLAT_DEV, TLON)
    return shaped.transpose(2, 3, 0, 4, 1, 5).reshape(VARS, LEV, 2 * CLAT, 2 * NLON)

def reference(members, alpha, zonal_loc, merid_coef, slot_tile, obs_count, obs_index, obs_value, obs_weight):
    band_ids = jnp.arange(BANDS, dtype=jnp.int32)[:, None, None]
    tile_ids = (band_ids * NTILE + slot_tile.astype(jnp.int32)) * TILE_CELLS
    global_points = (tile_ids[..., None] + obs_index.astype(jnp.int32)).reshape(-1)
    active = jnp.arange(OBS_TILE, dtype=jnp.int32)[None, None, None, :] < obs_count[..., None]
    current = alpha
    for iteration in range(ITERS):

        def add_member(running, member_pair):
            member_x, member_alpha = member_pair
            zonal_out = localize(member_alpha, merid_coef, zonal_loc)
            return (running + member_x.astype(jnp.float32) * zonal_out[None], None)
        increment, unused = lax.scan(add_member, jnp.zeros((VARS, LEV, CLAT, NLON), jnp.float32), (members, current))
        fine_field, pullback = jax.vjp(interpolate, increment)
        flat_tiles = to_tiles(fine_field)
        sampled = flat_tiles[global_points].reshape(obs_value.shape)
        residual = jnp.where(active, obs_weight * (sampled - obs_value), jnp.float32(0.0))
        fine_grad = jnp.zeros(flat_tiles.shape, jnp.float32).at[global_points].add(residual.reshape(-1))
        adjoint, = pullback(from_tiles(fine_grad))

        def member_grad(member_pair):
            member_x, member_alpha = member_pair
            weighted = lax.optimization_barrier(jnp.sum(member_x.astype(jnp.float32) * adjoint, axis=0)).astype(jnp.bfloat16)
            zonal_back = lax.dot_general(weighted.reshape(-1, NLON), zonal_loc, (((1,), (1,)), ((), ())), preferred_element_type=jnp.float32)
            return member_alpha + meridional_back(zonal_back.reshape(member_alpha.shape), merid_coef)
        gradient = lax.map(member_grad, (members, current))
        current = current - step_size * gradient
    return current
```

```python
import functools

import jax
import jax.numpy as jnp
from jax import lax
from jax.experimental import pallas as pl
from jax.experimental.pallas import tpu as pltpu
from jax.sharding import PartitionSpec as P

MESH = pl.DeviceIdType.MESH
ITERS = 2
HALF = 4
STEP = 0.3
F32 = jnp.float32
BF16 = jnp.bfloat16


def column_chunks(width):
    return [(at, min(256, width - at)) for at in range(0, width, 256)]


def kernel(
    dims,
    alpha_h, mem_h, z_h, coef_h, idx_h, val_h, wgt_h, tile_s, count_s, out_h,
    cur, mem, z, coef, idx, val, wgt,
    edge_out, halo, xp, lhs, inc_out, inc_in, line_out, line_in,
    obs_acc, obs_out, obs_in, placed, planes, rim_out, rim_in,
    adj_out, adj_in, adj, wsum, zp, out_v,
    local_sem, halo_send, halo_recv, obs_send, obs_recv, rim_send, rim_recv,
    inc_send, inc_recv, line_send, line_recv, adj_send, adj_recv, w_send, w_recv,
):
    members, variables, levels, cols, n_mem, n_lat, slots, n_obs = dims
    kl_count, vl_count = members * levels, variables * levels
    lane_tiles, tiles = cols // 128, cols // 64
    m, b = lax.axis_index("mem"), lax.axis_index("lat")
    north, south = lax.rem(b + 1, n_lat), lax.rem(b + n_lat - 1, n_lat)
    h = lax.rem(m, 2)
    mate = m + 1 - 2 * h
    strip_north = dict(mem=mate, lat=lax.rem(b + h, n_lat))
    strip_south = dict(mem=mate, lat=lax.rem(b + h + n_lat - 1, n_lat))
    strip = 2 * b + h

    def remote(src, dst, send, recv, to):
        return pltpu.make_async_remote_copy(
            src_ref=src, dst_ref=dst, send_sem=send, recv_sem=recv, device_id=to, device_id_type=MESH
        )

    loads = [
        pltpu.make_async_copy(src, dst, local_sem.at[i])
        for i, (src, dst) in enumerate(
            ((alpha_h, cur), (coef_h, coef), (idx_h, idx), (val_h, val), (wgt_h, wgt), (z_h, z), (mem_h, mem))
        )
    ]
    for copy in loads:
        copy.start()

    barrier = pltpu.get_barrier_semaphore()

    @pl.loop(0, n_mem - 1)
    def _(i):
        pl.semaphore_signal(
            barrier, 1, device_id=dict(mem=lax.rem(m + 1 + i, n_mem), lat=b), device_id_type=MESH
        )

    for to in (
        dict(mem=m, lat=north),
        dict(mem=m, lat=south),
        dict(mem=mate, lat=lax.rem(b + 2 * h + n_lat - 1, n_lat)),
    ):
        pl.semaphore_signal(barrier, 1, device_id=to, device_id_type=MESH)

    loads[0].wait()

    @pl.loop(0, kl_count)
    def _(kl):
        edge_out[0, kl] = cur[kl, 0:4]
        edge_out[1, kl] = cur[kl, 4:8]

    pl.semaphore_wait(barrier, n_mem + 2)
    halo_copies = [
        remote(edge_out.at[0], halo.at[1], halo_send.at[0], halo_recv.at[1], dict(mem=m, lat=south)),
        remote(edge_out.at[1], halo.at[0], halo_send.at[1], halo_recv.at[0], dict(mem=m, lat=north)),
    ]
    for copy in halo_copies:
        copy.start()

    @pl.loop(0, kl_count)
    def _(kl):
        for j in range(lane_tiles):
            xp[kl, j, 4:12, :] = cur[kl, :, 128 * j : 128 * j + 128]

    for copy in loads[1:5]:
        copy.wait()

    hot_rows = 16 * vl_count
    width = min(512, n_obs)
    row_at = lax.broadcasted_iota(jnp.int32, (hot_rows, width), 0)
    col_at = lax.broadcasted_iota(jnp.int32, (128, width), 0)
    for slot in range(slots):
        obs_acc[...] = jnp.zeros_like(obs_acc)

        @pl.loop(0, n_obs // width)
        def _(step):
            start = pl.multiple_of(step * width, width)
            points = idx[slot : slot + 1, pl.ds(start, width)]
            place = lax.broadcasted_iota(jnp.int32, (1, width), 1) + start
            live = place < count_s[slot]
            weight = jnp.where(live, wgt[slot : slot + 1, pl.ds(start, width)], 0.0)
            scaled = weight * val[slot : slot + 1, pl.ds(start, width)]
            row = lax.shift_right_logical(points, 7)
            row = (row & ~7) + (row & 1) * 4 + (lax.shift_right_logical(row, 1) & 3)
            col = (points & 1) * 64 + lax.shift_right_logical(points & 127, 1)
            in_row = row_at == row
            parts = []
            for amount in (weight, scaled):
                high = amount.astype(BF16).astype(F32)
                for part in (high, amount - high):
                    parts.append(jnp.where(in_row, part, 0.0).astype(BF16))
            hot = jnp.where(col_at == col, 1.0, 0.0).astype(BF16)
            obs_acc[...] += lax.dot_general(
                jnp.concatenate(parts, axis=0), hot, (((1,), (1,)), ((), ())), preferred_element_type=F32
            )

        for q in range(2):
            both = obs_acc[2 * q * hot_rows : (2 * q + 1) * hot_rows, :] + obs_acc[
                (2 * q + 1) * hot_rows : (2 * q + 2) * hot_rows, :
            ]
            obs_out[:, q * slots + slot] = both.reshape(n_mem, 8, 128)

    sub = lax.broadcasted_iota(jnp.int32, (8, 128), 0)
    ids = jnp.full((8, 128), -1.0, F32)
    for slot in range(slots):
        ids = jnp.where(sub == slot, jnp.full((8, 128), tile_s[slot], jnp.int32).astype(F32), ids)
    for d in range(n_mem):
        obs_out[d, 2 * slots] = ids

    def to_peers(i):
        return lax.rem(m + 1 + i, n_mem)

    def obs_copy(i):
        peer = to_peers(i)
        return remote(
            obs_out.at[peer], obs_in.at[m], obs_send.at[peer], obs_recv.at[m], dict(mem=peer, lat=b)
        )

    def obs_wait(i):
        peer = to_peers(i)
        return remote(
            obs_out.at[peer], obs_in.at[peer], obs_send.at[peer], obs_recv.at[peer], dict(mem=peer, lat=b)
        )

    @pl.loop(0, n_mem - 1)
    def _(i):
        obs_copy(i).start()

    obs_in[m] = obs_out[m]

    block = coef[pl.ds(pl.multiple_of(b * 8, 8), 32), :]
    row8 = lax.broadcasted_iota(jnp.int32, (8, 128), 0) + b * 8

    def coef_rows(first, s):
        return jnp.broadcast_to(block[first : first + 8, s : s + 1], (8, 128))

    def forward_coefs():
        out = []
        for s in range(2 * HALF + 1):
            reach = row8 + (s - HALF)
            out.append(jnp.where((reach >= 0) & (reach < 8 * n_lat), coef_rows(8, s), 0.0))
        return out

    def adjoint_coefs(first):
        return [coef_rows(8 + first - (s - HALF), s) for s in range(2 * HALF + 1)]

    for copy in halo_copies:
        copy.wait()

    @pl.loop(0, kl_count)
    def _(kl):
        for j in range(lane_tiles):
            xp[kl, j, 0:4, :] = halo[0, kl, :, 128 * j : 128 * j + 128]
            xp[kl, j, 12:16, :] = halo[1, kl, :, 128 * j : 128 * j + 128]

    for it in range(ITERS):
        fc = forward_coefs()

        @pl.loop(0, kl_count // 2)
        def _(pair):
            for j in range(lane_tiles):
                both = []
                for e in range(2):
                    total = jnp.zeros((8, 128), F32)
                    for s in range(2 * HALF + 1):
                        total = total + fc[s] * xp[2 * pair + e, j, s : s + 8, :]
                    both.append(total)
                lhs[pl.ds(pl.multiple_of(pair * 16, 16), 16), 128 * j : 128 * j + 128] = jnp.concatenate(
                    both, axis=0
                ).astype(BF16)

        if it == 0:
            loads[5].wait()
            loads[6].wait()
        for at, size in column_chunks(cols):
            local = jnp.dot(lhs[...], z[:, at : at + size], preferred_element_type=F32)
            for vl in range(vl_count):
                level = vl % levels
                total = jnp.zeros((8, size), F32)
                for k in range(members):
                    first = (k * levels + level) * 8
                    total = total + mem[k * vl_count + vl, :, at : at + size].astype(F32) * local[first : first + 8]
                inc_out[it, 2 * vl, :, at : at + size] = total[0:4]
                inc_out[it, 2 * vl + 1, :, at : at + size] = total[4:8]

        def inc_copy(i, mine):
            peer = to_peers(i)
            return remote(
                inc_out.at[it, peer], inc_in.at[it, m if mine else peer], inc_send.at[it, peer],
                inc_recv.at[it, m if mine else peer], dict(mem=peer, lat=b),
            )

        @pl.loop(0, n_mem - 1)
        def _(i):
            inc_copy(i, True).start()

        inc_in[it, m] = inc_out[it, m]

        if it == 0:

            @pl.loop(0, n_mem - 1)
            def _(i):
                obs_wait(i).wait()

            @pl.loop(0, tiles)
            def _(t):
                wanted = jnp.full((8, 128), t, jnp.int32).astype(F32)
                w_total = jnp.zeros((8, 128), F32)
                v_total = jnp.zeros((8, 128), F32)
                for src in range(n_mem):
                    for slot in range(slots):
                        here = jnp.broadcast_to(obs_in[src, 2 * slots, slot : slot + 1, :], (8, 128)) == wanted
                        w_total = w_total + jnp.where(here, obs_in[src, slot], 0.0)
                        v_total = v_total + jnp.where(here, obs_in[src, slots + slot], 0.0)
                placed[t, 0] = w_total
                placed[t, 1] = v_total

            low = lax.broadcasted_iota(jnp.int32, (8, 128), 1) < 64
            for u in range(lane_tiles):
                for q in range(2):
                    first, second = placed[2 * u, q], placed[2 * u + 1, q]
                    lanes = slice(128 * u, 128 * u + 128)
                    planes[2 * q, 0:8, lanes] = jnp.where(low, first, pltpu.roll(second, 64, 1))
                    planes[2 * q + 1, 0:8, lanes] = jnp.where(low, pltpu.roll(first, 64, 1), second)
            for q in range(4):
                planes[q, 8:16, :] = jnp.zeros((8, cols), F32)
                rim_out[0, q : q + 1, :] = planes[q, 0:1, :]
                rim_out[1, q : q + 1, :] = planes[q, 7:8, :]
            rim_copies = [
                remote(rim_out.at[0], rim_in.at[1], rim_send.at[0], rim_recv.at[1], strip_south),
                remote(rim_out.at[1], rim_in.at[0], rim_send.at[1], rim_recv.at[0], strip_north),
            ]
            for copy in rim_copies:
                copy.start()

        @pl.loop(0, n_mem - 1)
        def _(i):
            inc_copy(i, False).wait()

        inc = inc_in[it, 0]
        for src in range(1, n_mem):
            inc = inc + inc_in[it, src]
        line_out[it, 0] = inc[0:1]
        line_out[it, 1] = inc[3:4]
        line_copies = [
            remote(line_out.at[it, 0], line_in.at[it, 1], line_send.at[it, 0], line_recv.at[it, 1], strip_south),
            remote(line_out.at[it, 1], line_in.at[it, 0], line_send.at[it, 1], line_recv.at[it, 0], strip_north),
        ]
        for copy in line_copies:
            copy.start()
        at_south = strip == 0
        at_north = strip == 2 * n_lat - 1
        if it == 0:
            for copy in rim_copies:
                copy.wait()
            for q in range(4):
                planes[q, 8:9, :] = jnp.where(at_south, 0.0, rim_in[0, q : q + 1, :])
                planes[q, 9:10, :] = jnp.where(at_north, 0.0, rim_in[1, q : q + 1, :])
        for copy in line_copies:
            copy.wait()
        below = jnp.where(at_south, inc[0:1], line_in[it, 0])
        above = jnp.where(at_north, inc[3:4], line_in[it, 1])
        fine = jnp.concatenate(
            [
                0.75 * inc + 0.25 * jnp.concatenate([below, inc[0:3]], axis=0),
                0.75 * inc + 0.25 * jnp.concatenate([inc[1:4], above], axis=0),
                0.75 * below + 0.25 * inc[0:1],
                0.75 * above + 0.25 * inc[3:4],
                jnp.zeros((6, cols), F32),
            ],
            axis=0,
        )
        odd = 0.5 * (fine + pltpu.roll(fine, cols - 1, 1))
        even_res = planes[0] * fine - planes[2]
        odd_res = planes[1] * odd - planes[3]
        back = even_res + 0.5 * (odd_res + pltpu.roll(odd_res, 1, 1))
        row_even, row_odd = back[0:4], back[4:8]
        strip_adj = 0.75 * (row_even + row_odd) + 0.25 * (
            jnp.concatenate([row_even[1:4], back[9:10]], axis=0)
            + jnp.concatenate([back[8:9], row_odd[0:3]], axis=0)
        )
        row4 = lax.broadcasted_iota(jnp.int32, (4, cols), 0)
        strip_adj = strip_adj + jnp.where(at_south & (row4 == 0), 0.25 * row_even, 0.0)
        strip_adj = strip_adj + jnp.where(at_north & (row4 == 3), 0.25 * row_odd, 0.0)
        adj_out[it] = strip_adj

        def adj_copy(i, mine):
            peer = to_peers(i)
            return remote(
                adj_out.at[it], adj_in.at[it, m if mine else peer], adj_send.at[it, peer],
                adj_recv.at[it, m if mine else peer], dict(mem=peer, lat=b),
            )

        @pl.loop(0, n_mem - 1)
        def _(i):
            adj_copy(i, True).start()

        adj_in[it, m] = strip_adj

        @pl.loop(0, n_mem - 1)
        def _(i):
            adj_copy(i, False).wait()

        for vl in range(vl_count):
            adj[vl, 0:4] = adj_in[it, 2 * vl]
            adj[vl, 4:8] = adj_in[it, 2 * vl + 1]

        @pl.loop(0, members)
        def _(k):
            for pair in range(levels // 2):
                for j in range(lane_tiles):
                    lanes = slice(128 * j, 128 * j + 128)
                    both = []
                    for level in (2 * pair, 2 * pair + 1):
                        total = jnp.zeros((8, 128), F32)
                        for v in range(variables):
                            vl = v * levels + level
                            total = total + mem[k * vl_count + vl, :, lanes].astype(F32) * adj[vl, :, lanes]
                        both.append(total)
                    first = pl.multiple_of(k * levels * 8 + pair * 16, 16)
                    wsum[it, 1, pl.ds(first, 16), lanes] = jnp.concatenate(both, axis=0).astype(BF16)

        w_copies = [
            remote(wsum.at[it, 1], wsum.at[it, 2], w_send.at[it, 0], w_recv.at[it, 1], dict(mem=m, lat=south)),
            remote(wsum.at[it, 1], wsum.at[it, 0], w_send.at[it, 1], w_recv.at[it, 0], dict(mem=m, lat=north)),
        ]
        for copy in w_copies:
            copy.start()

        def zonal_back(segment):
            for at, size in column_chunks(cols):
                part = lax.dot_general(
                    wsum[it, segment], z[at : at + size, :], (((1,), (1,)), ((), ())), preferred_element_type=F32
                )
                part = part.reshape(kl_count, 8, size)
                for e in range(size // 128):
                    zp[:, at // 128 + e, 8 * segment : 8 * segment + 8, :] = part[:, :, 128 * e : 128 * e + 128]

        zonal_back(1)
        for copy in w_copies:
            copy.wait()
        zonal_back(0)
        zonal_back(2)

        if it < ITERS - 1:
            for part in range(2):
                bc = adjoint_coefs(8 * part - 4)

                @pl.loop(0, kl_count)
                def _(kl):
                    for j in range(lane_tiles):
                        here = xp[kl, j, 8 * part : 8 * part + 8, :]
                        total = jnp.zeros((8, 128), F32)
                        for s in range(2 * HALF + 1):
                            first = 8 * part + 8 - s
                            total = total + bc[s] * zp[kl, j, first : first + 8, :]
                        xp[kl, j, 8 * part : 8 * part + 8, :] = here - STEP * (here + total)
        else:
            bc = adjoint_coefs(0)

            @pl.loop(0, kl_count)
            def _(kl):
                for j in range(lane_tiles):
                    here = xp[kl, j, 4:12, :]
                    total = jnp.zeros((8, 128), F32)
                    for s in range(2 * HALF + 1):
                        total = total + bc[s] * zp[kl, j, 12 - s : 20 - s, :]
                    out_v[kl, :, 128 * j : 128 * j + 128] = here - STEP * (here + total)

    store = pltpu.make_async_copy(out_v, out_h, local_sem.at[0])
    store.start()
    store.wait()


def body(n_mem, n_lat, members, alpha, zonal_loc, merid_coef, slot_tile, obs_count, obs_index, obs_value, obs_weight):
    k, v, l, rows, cols = members.shape
    slots, n_obs = obs_index.shape[2:]
    kl, vl, lane_tiles = k * l, v * l, cols // 128
    dims = (k, v, l, cols, n_mem, n_lat, slots, n_obs)
    coef = jnp.pad(merid_coef, ((8, 16), (0, 0)))
    vmem, dma = pltpu.VMEM, pltpu.SemaphoreType.DMA
    out = pl.pallas_call(
        functools.partial(kernel, dims),
        out_shape=jax.ShapeDtypeStruct((kl, rows, cols), F32),
        in_specs=[pl.BlockSpec(memory_space=pl.ANY)] * 7 + [pl.BlockSpec(memory_space=pltpu.SMEM)] * 2,
        out_specs=pl.BlockSpec(memory_space=pl.ANY),
        scratch_shapes=[
            vmem((kl, rows, cols), F32),
            vmem((k * vl, rows, cols), BF16),
            vmem((cols, cols), BF16),
            vmem(coef.shape, F32),
            vmem((slots, n_obs), jnp.int32),
            vmem((slots, n_obs), F32),
            vmem((slots, n_obs), F32),
            vmem((2, kl, 4, cols), F32),
            vmem((2, kl, 4, cols), F32),
            vmem((kl, lane_tiles, 16, 128), F32),
            vmem((kl * rows, cols), BF16),
            vmem((ITERS, n_mem, 4, cols), F32),
            vmem((ITERS, n_mem, 4, cols), F32),
            vmem((ITERS, 2, 1, cols), F32),
            vmem((ITERS, 2, 1, cols), F32),
            vmem((64 * vl, 128), F32),
            vmem((n_mem, 2 * slots + 1, 8, 128), F32),
            vmem((n_mem, 2 * slots + 1, 8, 128), F32),
            vmem((2 * lane_tiles, 2, 8, 128), F32),
            vmem((4, 16, cols), F32),
            vmem((2, 4, cols), F32),
            vmem((2, 4, cols), F32),
            vmem((ITERS, 4, cols), F32),
            vmem((ITERS, n_mem, 4, cols), F32),
            vmem((vl, 8, cols), F32),
            vmem((ITERS, 3, kl * rows, cols), BF16),
            vmem((kl, lane_tiles, 24, 128), F32),
            vmem((kl, rows, cols), F32),
            dma((7,)),
            dma((2,)), dma((2,)),
            dma((n_mem,)), dma((n_mem,)),
            dma((2,)), dma((2,)),
            dma((ITERS, n_mem)), dma((ITERS, n_mem)),
            dma((ITERS, 2)), dma((ITERS, 2)),
            dma((ITERS, n_mem)), dma((ITERS, n_mem)),
            dma((ITERS, 2)), dma((ITERS, 2)),
        ],
        compiler_params=pltpu.CompilerParams(
            collective_id=0, has_side_effects=True, vmem_limit_bytes=60 * 1024 * 1024
        ),
    )(
        alpha.reshape(kl, rows, cols),
        members.reshape(k * vl, rows, cols),
        zonal_loc,
        coef,
        obs_index.reshape(slots, n_obs),
        obs_value.reshape(slots, n_obs),
        obs_weight.reshape(slots, n_obs),
        slot_tile.reshape(slots),
        obs_count.reshape(slots),
    )
    return out.reshape(alpha.shape)


def solution(mesh):
    in_specs = (
        P("mem", None, None, "lat", None),
        P("mem", None, "lat", None),
        P(),
        P(),
        P("lat", "mem", None),
        P("lat", "mem", None),
        P("lat", "mem", None, None),
        P("lat", "mem", None, None),
        P("lat", "mem", None, None),
    )
    step = functools.partial(body, mesh.shape["mem"], mesh.shape["lat"])
    return jax.shard_map(step, mesh=mesh, in_specs=in_specs, out_specs=P("mem", None, "lat", None), check_vma=False)
```

```python
import functools

import jax
import jax.numpy as jnp
from jax import lax
from jax.experimental import pallas as pl
from jax.experimental.pallas import tpu as pltpu
from jax.sharding import PartitionSpec as P

MESH = pl.DeviceIdType.MESH
ITERS = 2
HALF = 4
STEP = 0.3
F32 = jnp.float32
BF16 = jnp.bfloat16


def column_chunks(width):
    return [(at, min(256, width - at)) for at in range(0, width, 256)]


def kernel(
    dims,
    alpha_h, mem_h, z_h, coef_h, idx_h, val_h, wgt_h, tile_s, count_s, out_h,
    cur, mem, z, coef_in, coef, idx, val, wgt,
    edge_out, halo, xp, lhs, inc_out, inc_in, line_out, line_in,
    obs_acc, obs_out, obs_in, placed, planes, rim_out, rim_in,
    adj_out, adj_in, adj, w_out, w_in, w_in_last, zp, out_v,
    local_sem, store_sem, halo_send, halo_recv, obs_send, obs_recv, rim_send, rim_recv,
    inc_send, inc_recv, line_send, line_recv, adj_send, adj_recv, w_send, w_recv,
):
    members, variables, levels, cols, n_mem, n_lat, slots, n_obs = dims
    kl_count, vl_count = members * levels, variables * levels
    k_rows = levels * 8
    lane_tiles, tiles = cols // 128, cols // 64
    m, b = lax.axis_index("mem"), lax.axis_index("lat")
    north, south = lax.rem(b + 1, n_lat), lax.rem(b + n_lat - 1, n_lat)
    h = lax.rem(m, 2)
    mate = m + 1 - 2 * h
    strip_north = dict(mem=mate, lat=lax.rem(b + h, n_lat))
    strip_south = dict(mem=mate, lat=lax.rem(b + h + n_lat - 1, n_lat))
    strip = 2 * b + h

    def remote(src, dst, send, recv, to):
        return pltpu.make_async_remote_copy(
            src_ref=src, dst_ref=dst, send_sem=send, recv_sem=recv, device_id=to, device_id_type=MESH
        )

    loads = [
        pltpu.make_async_copy(src, dst, local_sem.at[i])
        for i, (src, dst) in enumerate(
            ((alpha_h, cur), (coef_h, coef_in), (idx_h, idx), (val_h, val), (wgt_h, wgt), (z_h, z), (mem_h, mem))
        )
    ]
    for copy in loads:
        copy.start()

    def store(k):
        part = pl.ds(k * levels, levels)
        return pltpu.make_async_copy(out_v.at[part], out_h.at[part], store_sem.at[k])

    barrier = pltpu.get_barrier_semaphore()

    @pl.loop(0, n_mem - 1)
    def _(i):
        pl.semaphore_signal(
            barrier, 1, device_id=dict(mem=lax.rem(m + 1 + i, n_mem), lat=b), device_id_type=MESH
        )

    for to in (
        dict(mem=m, lat=north),
        dict(mem=m, lat=south),
        dict(mem=mate, lat=lax.rem(b + 2 * h + n_lat - 1, n_lat)),
    ):
        pl.semaphore_signal(barrier, 1, device_id=to, device_id_type=MESH)

    loads[0].wait()

    @pl.loop(0, kl_count)
    def _(kl):
        edge_out[0, kl] = cur[kl, 0:4]
        edge_out[1, kl] = cur[kl, 4:8]

    pl.semaphore_wait(barrier, n_mem + 2)

    def halo_copies(k):
        part = pl.ds(k * levels, levels)
        return [
            remote(
                edge_out.at[0, part], halo.at[1, part], halo_send.at[0, k], halo_recv.at[1, k], dict(mem=m, lat=south)
            ),
            remote(
                edge_out.at[1, part], halo.at[0, part], halo_send.at[1, k], halo_recv.at[0, k], dict(mem=m, lat=north)
            ),
        ]

    @pl.loop(0, members)
    def _(k):
        for copy in halo_copies(k):
            copy.start()

    @pl.loop(0, kl_count)
    def _(kl):
        for j in range(lane_tiles):
            xp[kl, j, 4:12, :] = cur[kl, :, 128 * j : 128 * j + 128]

    for copy in loads[1:5]:
        copy.wait()

    hot_rows = 16 * vl_count
    width = min(512, n_obs)
    row_at = lax.broadcasted_iota(jnp.int32, (hot_rows, width), 0)
    col_at = lax.broadcasted_iota(jnp.int32, (128, width), 0)
    for slot in range(slots):
        obs_acc[...] = jnp.zeros_like(obs_acc)

        @pl.loop(0, n_obs // width)
        def _(step):
            start = pl.multiple_of(step * width, width)
            points = idx[slot, :, pl.ds(start, width)]
            place = lax.broadcasted_iota(jnp.int32, (1, width), 1) + start
            live = place < count_s[slot]
            weight = jnp.where(live, wgt[slot, :, pl.ds(start, width)], 0.0)
            scaled = weight * val[slot, :, pl.ds(start, width)]
            row = lax.shift_right_logical(points, 7)
            row = (row & ~7) + (row & 1) * 4 + (lax.shift_right_logical(row, 1) & 3)
            col = (points & 1) * 64 + lax.shift_right_logical(points & 127, 1)
            in_row = row_at == row
            parts = []
            for amount in (weight, scaled):
                high = amount.astype(BF16).astype(F32)
                for part in (high, amount - high):
                    parts.append(jnp.where(in_row, part, 0.0).astype(BF16))
            hot = jnp.where(col_at == col, 1.0, 0.0).astype(BF16)
            obs_acc[...] += lax.dot_general(
                jnp.concatenate(parts, axis=0), hot, (((1,), (1,)), ((), ())), preferred_element_type=F32
            )

        for q in range(2):
            both = obs_acc[2 * q * hot_rows : (2 * q + 1) * hot_rows, :] + obs_acc[
                (2 * q + 1) * hot_rows : (2 * q + 2) * hot_rows, :
            ]
            obs_out[:, q * slots + slot] = both.reshape(n_mem, 8, 128)

    sub = lax.broadcasted_iota(jnp.int32, (8, 128), 0)
    ids = jnp.full((8, 128), -1.0, F32)
    for slot in range(slots):
        ids = jnp.where(sub == slot, jnp.full((8, 128), tile_s[slot], jnp.int32).astype(F32), ids)
    for d in range(n_mem):
        obs_out[d, 2 * slots] = ids

    def to_peers(i):
        return lax.rem(m + 1 + i, n_mem)

    def obs_copy(i):
        peer = to_peers(i)
        return remote(
            obs_out.at[peer], obs_in.at[m], obs_send.at[peer], obs_recv.at[m], dict(mem=peer, lat=b)
        )

    def obs_wait(i):
        peer = to_peers(i)
        return remote(
            obs_out.at[peer], obs_in.at[peer], obs_send.at[peer], obs_recv.at[peer], dict(mem=peer, lat=b)
        )

    @pl.loop(0, n_mem - 1)
    def _(i):
        obs_copy(i).start()

    obs_in[m] = obs_out[m]

    grid_rows, taps = coef_in.shape[1], coef_in.shape[0]
    coef[...] = jnp.zeros_like(coef)
    coef[8 : 8 + grid_rows, :] = jnp.concatenate(
        [coef_in[...], jnp.zeros((128 - taps, grid_rows), F32)], axis=0
    ).T
    block = coef[pl.ds(pl.multiple_of(b * 8, 8), 32), :]
    row8 = lax.broadcasted_iota(jnp.int32, (8, 128), 0) + b * 8

    def coef_rows(first, s):
        return jnp.broadcast_to(block[first : first + 8, s : s + 1], (8, 128))

    def forward_coefs():
        out = []
        for s in range(2 * HALF + 1):
            reach = row8 + (s - HALF)
            out.append(jnp.where((reach >= 0) & (reach < 8 * n_lat), coef_rows(8, s), 0.0))
        return out

    def adjoint_coefs(first):
        return [coef_rows(8 + first - (s - HALF), s) for s in range(2 * HALF + 1)]

    def spread_rows(k):
        fc = forward_coefs()

        @pl.loop(0, levels // 2)
        def _(pair):
            for j in range(lane_tiles):
                both = []
                for e in range(2):
                    total = jnp.zeros((8, 128), F32)
                    for s in range(2 * HALF + 1):
                        total = total + fc[s] * xp[k * levels + 2 * pair + e, j, s : s + 8, :]
                    both.append(total)
                first = pl.multiple_of(k * k_rows + pair * 16, 16)
                lhs[pl.ds(first, 16), 128 * j : 128 * j + 128] = jnp.concatenate(both, axis=0).astype(BF16)

    @pl.loop(0, members)
    def _(k):
        for copy in halo_copies(k):
            copy.wait()

        @pl.loop(0, levels)
        def _(level):
            kl = k * levels + level
            for j in range(lane_tiles):
                xp[kl, j, 0:4, :] = halo[0, kl, :, 128 * j : 128 * j + 128]
                xp[kl, j, 12:16, :] = halo[1, kl, :, 128 * j : 128 * j + 128]

        spread_rows(k)

    for it in range(ITERS):
        last = it == ITERS - 1
        if it == 0:
            loads[5].wait()
            loads[6].wait()
        for at, size in column_chunks(cols):
            local = jnp.dot(lhs[...], z[:, at : at + size], preferred_element_type=F32)
            for vl in range(vl_count):
                level = vl % levels
                total = jnp.zeros((8, size), F32)
                for k in range(members):
                    first = (k * levels + level) * 8
                    total = total + mem[k * vl_count + vl, :, at : at + size].astype(F32) * local[first : first + 8]
                inc_out[it, 2 * vl, :, at : at + size] = total[0:4]
                inc_out[it, 2 * vl + 1, :, at : at + size] = total[4:8]

        def inc_copy(i, mine):
            peer = to_peers(i)
            return remote(
                inc_out.at[it, peer], inc_in.at[it, m if mine else peer], inc_send.at[it, peer],
                inc_recv.at[it, m if mine else peer], dict(mem=peer, lat=b),
            )

        @pl.loop(0, n_mem - 1)
        def _(i):
            inc_copy(i, True).start()

        inc_in[it, m] = inc_out[it, m]

        if it == 0:

            @pl.loop(0, n_mem - 1)
            def _(i):
                obs_wait(i).wait()

            @pl.loop(0, tiles)
            def _(t):
                wanted = jnp.full((8, 128), t, jnp.int32).astype(F32)
                w_total = jnp.zeros((8, 128), F32)
                v_total = jnp.zeros((8, 128), F32)
                for src in range(n_mem):
                    for slot in range(slots):
                        here = jnp.broadcast_to(obs_in[src, 2 * slots, slot : slot + 1, :], (8, 128)) == wanted
                        w_total = w_total + jnp.where(here, obs_in[src, slot], 0.0)
                        v_total = v_total + jnp.where(here, obs_in[src, slots + slot], 0.0)
                placed[t, 0] = w_total
                placed[t, 1] = v_total

            low = lax.broadcasted_iota(jnp.int32, (8, 128), 1) < 64
            for u in range(lane_tiles):
                for q in range(2):
                    first, second = placed[2 * u, q], placed[2 * u + 1, q]
                    lanes = slice(128 * u, 128 * u + 128)
                    planes[2 * q, 0:8, lanes] = jnp.where(low, first, pltpu.roll(second, 64, 1))
                    planes[2 * q + 1, 0:8, lanes] = jnp.where(low, pltpu.roll(first, 64, 1), second)
            for q in range(4):
                planes[q, 8:16, :] = jnp.zeros((8, cols), F32)
                rim_out[0, q : q + 1, :] = planes[q, 0:1, :]
                rim_out[1, q : q + 1, :] = planes[q, 7:8, :]
            rim_copies = [
                remote(rim_out.at[0], rim_in.at[1], rim_send.at[0], rim_recv.at[1], strip_south),
                remote(rim_out.at[1], rim_in.at[0], rim_send.at[1], rim_recv.at[0], strip_north),
            ]
            for copy in rim_copies:
                copy.start()

        @pl.loop(0, n_mem - 1)
        def _(i):
            inc_copy(i, False).wait()

        inc = inc_in[it, 0]
        for src in range(1, n_mem):
            inc = inc + inc_in[it, src]
        line_out[it, 0] = inc[0:1]
        line_out[it, 1] = inc[3:4]
        line_copies = [
            remote(line_out.at[it, 0], line_in.at[it, 1], line_send.at[it, 0], line_recv.at[it, 1], strip_south),
            remote(line_out.at[it, 1], line_in.at[it, 0], line_send.at[it, 1], line_recv.at[it, 0], strip_north),
        ]
        for copy in line_copies:
            copy.start()
        at_south = strip == 0
        at_north = strip == 2 * n_lat - 1
        if it == 0:
            for copy in rim_copies:
                copy.wait()
            for q in range(4):
                planes[q, 8:9, :] = jnp.where(at_south, 0.0, rim_in[0, q : q + 1, :])
                planes[q, 9:10, :] = jnp.where(at_north, 0.0, rim_in[1, q : q + 1, :])
        for copy in line_copies:
            copy.wait()
        below = jnp.where(at_south, inc[0:1], line_in[it, 0])
        above = jnp.where(at_north, inc[3:4], line_in[it, 1])
        fine = jnp.concatenate(
            [
                0.75 * inc + 0.25 * jnp.concatenate([below, inc[0:3]], axis=0),
                0.75 * inc + 0.25 * jnp.concatenate([inc[1:4], above], axis=0),
                0.75 * below + 0.25 * inc[0:1],
                0.75 * above + 0.25 * inc[3:4],
                jnp.zeros((6, cols), F32),
            ],
            axis=0,
        )
        odd = 0.5 * (fine + pltpu.roll(fine, cols - 1, 1))
        even_res = planes[0] * fine - planes[2]
        odd_res = planes[1] * odd - planes[3]
        back = even_res + 0.5 * (odd_res + pltpu.roll(odd_res, 1, 1))
        row_even, row_odd = back[0:4], back[4:8]
        strip_adj = 0.75 * (row_even + row_odd) + 0.25 * (
            jnp.concatenate([row_even[1:4], back[9:10]], axis=0)
            + jnp.concatenate([back[8:9], row_odd[0:3]], axis=0)
        )
        row4 = lax.broadcasted_iota(jnp.int32, (4, cols), 0)
        strip_adj = strip_adj + jnp.where(at_south & (row4 == 0), 0.25 * row_even, 0.0)
        strip_adj = strip_adj + jnp.where(at_north & (row4 == 3), 0.25 * row_odd, 0.0)
        adj_out[it] = strip_adj

        def adj_copy(i, mine):
            peer = to_peers(i)
            return remote(
                adj_out.at[it], adj_in.at[it, m if mine else peer], adj_send.at[it, peer],
                adj_recv.at[it, m if mine else peer], dict(mem=peer, lat=b),
            )

        @pl.loop(0, n_mem - 1)
        def _(i):
            adj_copy(i, True).start()

        adj_in[it, m] = strip_adj

        @pl.loop(0, n_mem - 1)
        def _(i):
            adj_copy(i, False).wait()

        for vl in range(vl_count):
            adj[vl, 0:4] = adj_in[it, 2 * vl]
            adj[vl, 4:8] = adj_in[it, 2 * vl + 1]

        w_from = w_in_last if last else w_in

        def w_copies(k):
            lower, upper = (w_out.at[it, k, 0:16], w_out.at[it, k, 16:32]) if last else (w_out.at[it, k],) * 2
            half = lower.shape[0]
            return [
                remote(
                    lower, w_from.at[k, half : 2 * half], w_send.at[it, 0, k], w_recv.at[it, 1, k],
                    dict(mem=m, lat=south),
                ),
                remote(
                    upper, w_from.at[k, 0:half], w_send.at[it, 1, k], w_recv.at[it, 0, k], dict(mem=m, lat=north)
                ),
            ]

        @pl.loop(0, members)
        def _(k):
            for j in range(lane_tiles):
                lanes = slice(128 * j, 128 * j + 128)
                rows = []
                for level in range(levels):
                    total = jnp.zeros((8, 128), F32)
                    for v in range(variables):
                        vl = v * levels + level
                        total = total + mem[k * vl_count + vl, :, lanes].astype(F32) * adj[vl, :, lanes]
                    rows.append(total)
                if last:
                    rows = [r[0:4] for r in rows] + [r[4:8] for r in rows]
                w_out[it, k, :, lanes] = jnp.concatenate(rows, axis=0).astype(BF16)
            for copy in w_copies(k):
                copy.start()

        def zonal_product(rows, store):
            for at, size in column_chunks(cols):
                part = lax.dot_general(
                    rows, z[at : at + size, :], (((1,), (1,)), ((), ())), preferred_element_type=F32
                )
                for e in range(size // 128):
                    store(at // 128 + e, part[:, 128 * e : 128 * e + 128])

        def own_rows(j, part):
            for k in range(members):
                for level in range(levels):
                    kl, first = k * levels + level, k * k_rows
                    if last:
                        zp[kl, j, 8:12, :] = part[first + 4 * level : first + 4 * level + 4]
                        first += k_rows // 2
                        zp[kl, j, 12:16, :] = part[first + 4 * level : first + 4 * level + 4]
                    else:
                        zp[kl, j, 8:16, :] = part[first + 8 * level : first + 8 * level + 8]

        zonal_product(w_out[it].reshape(members * k_rows, cols), own_rows)

        coefs = [adjoint_coefs(0)] if last else [adjoint_coefs(-4), adjoint_coefs(4)]

        @pl.loop(0, members)
        def _(k):
            for copy in w_copies(k):
                copy.wait()

            def neighbour_rows(j, part):
                for level in range(levels):
                    kl = k * levels + level
                    if last:
                        zp[kl, j, 4:8, :] = part[4 * level : 4 * level + 4]
                        zp[kl, j, 16:20, :] = part[16 + 4 * level : 20 + 4 * level]
                    else:
                        zp[kl, j, 0:8, :] = part[8 * level : 8 * level + 8]
                        zp[kl, j, 16:24, :] = part[k_rows + 8 * level : k_rows + 8 * level + 8]

            zonal_product(w_from[k], neighbour_rows)

            if last:

                @pl.loop(0, levels)
                def _(level):
                    kl = k * levels + level
                    for j in range(lane_tiles):
                        here = xp[kl, j, 4:12, :]
                        total = jnp.zeros((8, 128), F32)
                        for s in range(2 * HALF + 1):
                            total = total + coefs[0][s] * zp[kl, j, 12 - s : 20 - s, :]
                        out_v[kl, :, 128 * j : 128 * j + 128] = here - STEP * (here + total)

                store(k).start()
            else:
                for part in range(2):

                    @pl.loop(0, levels)
                    def _(level):
                        kl = k * levels + level
                        for j in range(lane_tiles):
                            here = xp[kl, j, 8 * part : 8 * part + 8, :]
                            total = jnp.zeros((8, 128), F32)
                            for s in range(2 * HALF + 1):
                                first = 8 * part + 8 - s
                                total = total + coefs[part][s] * zp[kl, j, first : first + 8, :]
                            xp[kl, j, 8 * part : 8 * part + 8, :] = here - STEP * (here + total)

                spread_rows(k)

    @pl.loop(0, members)
    def _(k):
        store(k).wait()


def body(n_mem, n_lat, members, alpha, zonal_loc, merid_coef, slot_tile, obs_count, obs_index, obs_value, obs_weight):
    k, v, l, rows, cols = members.shape
    slots, n_obs = obs_index.shape[2:]
    kl, vl, lane_tiles = k * l, v * l, cols // 128
    dims = (k, v, l, cols, n_mem, n_lat, slots, n_obs)
    n_taps = merid_coef.shape[1]
    vmem, dma = pltpu.VMEM, pltpu.SemaphoreType.DMA

    def by_slot(array):
        return array.transpose(0, 2, 1, 3).reshape(slots, 1, n_obs)

    out = pl.pallas_call(
        functools.partial(kernel, dims),
        out_shape=jax.ShapeDtypeStruct((kl, rows, cols), F32),
        in_specs=[pl.BlockSpec(memory_space=pl.ANY)] * 7 + [pl.BlockSpec(memory_space=pltpu.SMEM)] * 2,
        out_specs=pl.BlockSpec(memory_space=pl.ANY),
        scratch_shapes=[
            vmem((kl, rows, cols), F32),
            vmem((k * vl, rows, cols), BF16),
            vmem((cols, cols), BF16),
            vmem((n_taps, n_lat * rows), F32),
            vmem((n_lat * rows + 24, 128), F32),
            vmem((slots, 1, n_obs), jnp.int32),
            vmem((slots, 1, n_obs), F32),
            vmem((slots, 1, n_obs), F32),
            vmem((2, kl, 4, cols), F32),
            vmem((2, kl, 4, cols), F32),
            vmem((kl, lane_tiles, 16, 128), F32),
            vmem((kl * rows, cols), BF16),
            vmem((ITERS, n_mem, 4, cols), F32),
            vmem((ITERS, n_mem, 4, cols), F32),
            vmem((ITERS, 2, 1, cols), F32),
            vmem((ITERS, 2, 1, cols), F32),
            vmem((64 * vl, 128), F32),
            vmem((n_mem, 2 * slots + 1, 8, 128), F32),
            vmem((n_mem, 2 * slots + 1, 8, 128), F32),
            vmem((2 * lane_tiles, 2, 8, 128), F32),
            vmem((4, 16, cols), F32),
            vmem((2, 4, cols), F32),
            vmem((2, 4, cols), F32),
            vmem((ITERS, 4, cols), F32),
            vmem((ITERS, n_mem, 4, cols), F32),
            vmem((vl, 8, cols), F32),
            vmem((ITERS, k, l * rows, cols), BF16),
            vmem((k, 2 * l * rows, cols), BF16),
            vmem((k, l * rows, cols), BF16),
            vmem((kl, lane_tiles, 24, 128), F32),
            vmem((kl, rows, cols), F32),
            dma((7,)), dma((k,)),
            dma((2, k)), dma((2, k)),
            dma((n_mem,)), dma((n_mem,)),
            dma((2,)), dma((2,)),
            dma((ITERS, n_mem)), dma((ITERS, n_mem)),
            dma((ITERS, 2)), dma((ITERS, 2)),
            dma((ITERS, n_mem)), dma((ITERS, n_mem)),
            dma((ITERS, 2, k)), dma((ITERS, 2, k)),
        ],
        compiler_params=pltpu.CompilerParams(
            collective_id=0, has_side_effects=True, vmem_limit_bytes=60 * 1024 * 1024
        ),
    )(
        alpha.reshape(kl, rows, cols),
        members.reshape(k * vl, rows, cols),
        zonal_loc,
        merid_coef.T,
        by_slot(obs_index),
        by_slot(obs_value),
        by_slot(obs_weight),
        slot_tile.reshape(slots),
        obs_count.reshape(slots),
    )
    return out.reshape(alpha.shape)


def solution(mesh):
    in_specs = (
        P("mem", None, None, "lat", None),
        P("mem", None, "lat", None),
        P(),
        P(),
        P("lat", "mem", None),
        P("lat", "mem", None),
        P("lat", "mem", None, None),
        P("lat", "mem", None, None),
        P("lat", "mem", None, None),
    )
    step = functools.partial(body, mesh.shape["mem"], mesh.shape["lat"])
    return jax.shard_map(step, mesh=mesh, in_specs=in_specs, out_specs=P("mem", None, "lat", None), check_vma=False)
```

```python
import functools

import jax
import jax.numpy as jnp
from jax import lax
from jax.experimental import pallas as pl
from jax.experimental.pallas import tpu as pltpu
from jax.sharding import PartitionSpec as P

MESH = pl.DeviceIdType.MESH
ITERS = 2
HALF = 4
STEP = 0.3
F32 = jnp.float32
BF16 = jnp.bfloat16


def column_chunks(width):
    return [(at, min(256, width - at)) for at in range(0, width, 256)]


def kernel(
    dims,
    alpha_h, mem_h, z_h, coef_h, idx_h, val_h, wgt_h, tile_s, count_s, out_h,
    cur, mem, z, z_t, coef_in, coef, idx, val, wgt,
    edge_out, halo, xp, lhs, inc_out, inc_in, line_out, line_in,
    obs_acc, obs_out, obs_in, placed, planes, rim_out, rim_in,
    adj_out, adj_in, adj, w_out, w_in, w_in_last, zp, out_v,
    local_sem, store_sem, halo_send, halo_recv, obs_send, obs_recv, rim_send, rim_recv,
    inc_send, inc_recv, line_send, line_recv, adj_send, adj_recv, w_send, w_recv,
):
    members, variables, levels, cols, n_mem, n_lat, slots, n_obs = dims
    kl_count, vl_count = members * levels, variables * levels
    k_rows = levels * 8
    lane_tiles, tiles = cols // 128, cols // 64
    m, b = lax.axis_index("mem"), lax.axis_index("lat")
    north, south = lax.rem(b + 1, n_lat), lax.rem(b + n_lat - 1, n_lat)
    h = lax.rem(m, 2)
    mate = m + 1 - 2 * h
    group = n_mem // 2
    x_half = lax.rem(lax.div(m, 2), 2)
    spot = lax.div(m, 4) * 2 + h
    across = m + 2 - 4 * x_half

    def near(i):
        other = lax.rem(spot + 1 + i, group)
        return other, lax.div(other, 2) * 4 + x_half * 2 + lax.rem(other, 2)

    def far(peer):
        return peer + 2 - 4 * x_half

    strip_north = dict(mem=mate, lat=lax.rem(b + h, n_lat))
    strip_south = dict(mem=mate, lat=lax.rem(b + h + n_lat - 1, n_lat))
    strip = 2 * b + h

    def remote(src, dst, send, recv, to):
        return pltpu.make_async_remote_copy(
            src_ref=src, dst_ref=dst, send_sem=send, recv_sem=recv, device_id=to, device_id_type=MESH
        )

    loads = [
        pltpu.make_async_copy(src, dst, local_sem.at[i])
        for i, (src, dst) in enumerate(
            ((alpha_h, cur), (coef_h, coef_in), (idx_h, idx), (val_h, val), (wgt_h, wgt), (z_h, z), (mem_h, mem))
        )
    ]
    for copy in loads:
        copy.start()

    def store(k):
        part = pl.ds(k * levels, levels)
        return pltpu.make_async_copy(out_v.at[part], out_h.at[part], store_sem.at[k])

    barrier = pltpu.get_barrier_semaphore()

    @pl.loop(0, n_mem - 1)
    def _(i):
        pl.semaphore_signal(
            barrier, 1, device_id=dict(mem=lax.rem(m + 1 + i, n_mem), lat=b), device_id_type=MESH
        )

    for to in (
        dict(mem=m, lat=north),
        dict(mem=m, lat=south),
        dict(mem=mate, lat=lax.rem(b + 2 * h + n_lat - 1, n_lat)),
    ):
        pl.semaphore_signal(barrier, 1, device_id=to, device_id_type=MESH)

    loads[0].wait()

    @pl.loop(0, kl_count)
    def _(kl):
        edge_out[0, kl] = cur[kl, 0:4]
        edge_out[1, kl] = cur[kl, 4:8]

    pl.semaphore_wait(barrier, n_mem + 2)

    def halo_copies(k):
        part = pl.ds(k * levels, levels)
        return [
            remote(
                edge_out.at[0, part], halo.at[1, part], halo_send.at[0, k], halo_recv.at[1, k], dict(mem=m, lat=south)
            ),
            remote(
                edge_out.at[1, part], halo.at[0, part], halo_send.at[1, k], halo_recv.at[0, k], dict(mem=m, lat=north)
            ),
        ]

    @pl.loop(0, members)
    def _(k):
        for copy in halo_copies(k):
            copy.start()

    @pl.loop(0, kl_count)
    def _(kl):
        for j in range(lane_tiles):
            xp[kl, j, 4:12, :] = cur[kl, :, 128 * j : 128 * j + 128]

    for copy in loads[1:5]:
        copy.wait()

    hot_rows = 16 * vl_count
    width = min(512, n_obs)
    row_at = lax.broadcasted_iota(jnp.int32, (hot_rows, width), 0)
    col_at = lax.broadcasted_iota(jnp.int32, (128, width), 0)
    for slot in range(slots):
        obs_acc[...] = jnp.zeros_like(obs_acc)

        @pl.loop(0, n_obs // width)
        def _(step):
            start = pl.multiple_of(step * width, width)
            points = idx[slot, :, pl.ds(start, width)]
            place = lax.broadcasted_iota(jnp.int32, (1, width), 1) + start
            live = place < count_s[slot]
            weight = jnp.where(live, wgt[slot, :, pl.ds(start, width)], 0.0)
            scaled = weight * val[slot, :, pl.ds(start, width)]
            row = lax.shift_right_logical(points, 7)
            row = (row & ~7) + (row & 1) * 4 + (lax.shift_right_logical(row, 1) & 3)
            col = (points & 1) * 64 + lax.shift_right_logical(points & 127, 1)
            in_row = row_at == row
            parts = []
            for amount in (weight, scaled):
                high = amount.astype(BF16).astype(F32)
                for part in (high, amount - high):
                    parts.append(jnp.where(in_row, part, 0.0).astype(BF16))
            hot = jnp.where(col_at == col, 1.0, 0.0).astype(BF16)
            obs_acc[...] += lax.dot_general(
                jnp.concatenate(parts, axis=0), hot, (((1,), (1,)), ((), ())), preferred_element_type=F32
            )

        for q in range(2):
            both = obs_acc[2 * q * hot_rows : (2 * q + 1) * hot_rows, :] + obs_acc[
                (2 * q + 1) * hot_rows : (2 * q + 2) * hot_rows, :
            ]
            obs_out[:, q * slots + slot] = both.reshape(n_mem, 8, 128)

    sub = lax.broadcasted_iota(jnp.int32, (8, 128), 0)
    ids = jnp.full((8, 128), -1.0, F32)
    for slot in range(slots):
        ids = jnp.where(sub == slot, jnp.full((8, 128), tile_s[slot], jnp.int32).astype(F32), ids)
    for d in range(n_mem):
        obs_out[d, 2 * slots] = ids

    def to_peers(i):
        return lax.rem(m + 1 + i, n_mem)

    def obs_copy(i):
        peer = to_peers(i)
        return remote(
            obs_out.at[peer], obs_in.at[m], obs_send.at[peer], obs_recv.at[m], dict(mem=peer, lat=b)
        )

    def obs_wait(i):
        peer = to_peers(i)
        return remote(
            obs_out.at[peer], obs_in.at[peer], obs_send.at[peer], obs_recv.at[peer], dict(mem=peer, lat=b)
        )

    @pl.loop(0, n_mem - 1)
    def _(i):
        obs_copy(i).start()

    obs_in[m] = obs_out[m]

    loads[5].wait()
    for at, size in column_chunks(cols):
        z_t[:, at : at + size] = z[at : at + size, :].T

    grid_rows, taps = coef_in.shape[1], coef_in.shape[0]
    coef[...] = jnp.zeros_like(coef)
    coef[8 : 8 + grid_rows, :] = jnp.concatenate(
        [coef_in[...], jnp.zeros((128 - taps, grid_rows), F32)], axis=0
    ).T
    block = coef[pl.ds(pl.multiple_of(b * 8, 8), 32), :]
    row8 = lax.broadcasted_iota(jnp.int32, (8, 128), 0) + b * 8

    def coef_rows(first, s):
        return jnp.broadcast_to(block[first : first + 8, s : s + 1], (8, 128))

    def forward_coefs():
        out = []
        for s in range(2 * HALF + 1):
            reach = row8 + (s - HALF)
            out.append(jnp.where((reach >= 0) & (reach < 8 * n_lat), coef_rows(8, s), 0.0))
        return out

    def adjoint_coefs(first):
        return [coef_rows(8 + first - (s - HALF), s) for s in range(2 * HALF + 1)]

    def spread_rows(k):
        fc = forward_coefs()

        @pl.loop(0, levels // 2)
        def _(pair):
            for j in range(lane_tiles):
                both = []
                for e in range(2):
                    total = jnp.zeros((8, 128), F32)
                    for s in range(2 * HALF + 1):
                        total = total + fc[s] * xp[k * levels + 2 * pair + e, j, s : s + 8, :]
                    both.append(total)
                first = pl.multiple_of(k * k_rows + pair * 16, 16)
                lhs[pl.ds(first, 16), 128 * j : 128 * j + 128] = jnp.concatenate(both, axis=0).astype(BF16)

    @pl.loop(0, members)
    def _(k):
        for copy in halo_copies(k):
            copy.wait()

        @pl.loop(0, levels)
        def _(level):
            kl = k * levels + level
            for j in range(lane_tiles):
                xp[kl, j, 0:4, :] = halo[0, kl, :, 128 * j : 128 * j + 128]
                xp[kl, j, 12:16, :] = halo[1, kl, :, 128 * j : 128 * j + 128]

        spread_rows(k)

    for it in range(ITERS):
        last = it == ITERS - 1
        if it == 0:
            loads[6].wait()
        for at, size in column_chunks(cols):
            local = jnp.dot(lhs[...], z[:, at : at + size], preferred_element_type=F32)
            for vl in range(vl_count):
                level = vl % levels
                total = jnp.zeros((8, size), F32)
                for k in range(members):
                    first = (k * levels + level) * 8
                    total = total + mem[k * vl_count + vl, :, at : at + size].astype(F32) * local[first : first + 8]
                inc_out[it, 2 * vl, :, at : at + size] = total[0:4]
                inc_out[it, 2 * vl + 1, :, at : at + size] = total[4:8]

        def inc_copy(i, mine):
            peer = to_peers(i)
            return remote(
                inc_out.at[it, peer], inc_in.at[it, m if mine else peer], inc_send.at[it, peer],
                inc_recv.at[it, m if mine else peer], dict(mem=peer, lat=b),
            )

        @pl.loop(0, n_mem - 1)
        def _(i):
            inc_copy(i, True).start()

        inc_in[it, m] = inc_out[it, m]

        if it == 0:

            @pl.loop(0, n_mem - 1)
            def _(i):
                obs_wait(i).wait()

            @pl.loop(0, tiles)
            def _(t):
                wanted = jnp.full((8, 128), t, jnp.int32).astype(F32)
                w_total = jnp.zeros((8, 128), F32)
                v_total = jnp.zeros((8, 128), F32)
                for src in range(n_mem):
                    for slot in range(slots):
                        here = jnp.broadcast_to(obs_in[src, 2 * slots, slot : slot + 1, :], (8, 128)) == wanted
                        w_total = w_total + jnp.where(here, obs_in[src, slot], 0.0)
                        v_total = v_total + jnp.where(here, obs_in[src, slots + slot], 0.0)
                placed[t, 0] = w_total
                placed[t, 1] = v_total

            low = lax.broadcasted_iota(jnp.int32, (8, 128), 1) < 64
            for u in range(lane_tiles):
                for q in range(2):
                    first, second = placed[2 * u, q], placed[2 * u + 1, q]
                    lanes = slice(128 * u, 128 * u + 128)
                    planes[2 * q, 0:8, lanes] = jnp.where(low, first, pltpu.roll(second, 64, 1))
                    planes[2 * q + 1, 0:8, lanes] = jnp.where(low, pltpu.roll(first, 64, 1), second)
            for q in range(4):
                planes[q, 8:16, :] = jnp.zeros((8, cols), F32)
                rim_out[0, q : q + 1, :] = planes[q, 0:1, :]
                rim_out[1, q : q + 1, :] = planes[q, 7:8, :]
            rim_copies = [
                remote(rim_out.at[0], rim_in.at[1], rim_send.at[0], rim_recv.at[1], strip_south),
                remote(rim_out.at[1], rim_in.at[0], rim_send.at[1], rim_recv.at[0], strip_north),
            ]
            for copy in rim_copies:
                copy.start()

        @pl.loop(0, n_mem - 1)
        def _(i):
            inc_copy(i, False).wait()

        inc = inc_in[it, 0]
        for src in range(1, n_mem):
            inc = inc + inc_in[it, src]
        line_out[it, 0] = inc[0:1]
        line_out[it, 1] = inc[3:4]
        line_copies = [
            remote(line_out.at[it, 0], line_in.at[it, 1], line_send.at[it, 0], line_recv.at[it, 1], strip_south),
            remote(line_out.at[it, 1], line_in.at[it, 0], line_send.at[it, 1], line_recv.at[it, 0], strip_north),
        ]
        for copy in line_copies:
            copy.start()
        at_south = strip == 0
        at_north = strip == 2 * n_lat - 1
        if it == 0:
            for copy in rim_copies:
                copy.wait()
            for q in range(4):
                planes[q, 8:9, :] = jnp.where(at_south, 0.0, rim_in[0, q : q + 1, :])
                planes[q, 9:10, :] = jnp.where(at_north, 0.0, rim_in[1, q : q + 1, :])
        for copy in line_copies:
            copy.wait()
        below = jnp.where(at_south, inc[0:1], line_in[it, 0])
        above = jnp.where(at_north, inc[3:4], line_in[it, 1])
        fine = jnp.concatenate(
            [
                0.75 * inc + 0.25 * jnp.concatenate([below, inc[0:3]], axis=0),
                0.75 * inc + 0.25 * jnp.concatenate([inc[1:4], above], axis=0),
                0.75 * below + 0.25 * inc[0:1],
                0.75 * above + 0.25 * inc[3:4],
                jnp.zeros((6, cols), F32),
            ],
            axis=0,
        )
        odd = 0.5 * (fine + pltpu.roll(fine, cols - 1, 1))
        even_res = planes[0] * fine - planes[2]
        odd_res = planes[1] * odd - planes[3]
        back = even_res + 0.5 * (odd_res + pltpu.roll(odd_res, 1, 1))
        row_even, row_odd = back[0:4], back[4:8]
        strip_adj = 0.75 * (row_even + row_odd) + 0.25 * (
            jnp.concatenate([row_even[1:4], back[9:10]], axis=0)
            + jnp.concatenate([back[8:9], row_odd[0:3]], axis=0)
        )
        row4 = lax.broadcasted_iota(jnp.int32, (4, cols), 0)
        strip_adj = strip_adj + jnp.where(at_south & (row4 == 0), 0.25 * row_even, 0.0)
        strip_adj = strip_adj + jnp.where(at_north & (row4 == 3), 0.25 * row_odd, 0.0)
        adj_out[it] = strip_adj

        def adj_copy(i, owner, mine):
            peer = near(i)[1]
            own = owner == 0
            mark = (m if own else across) if mine else (peer if own else far(peer))
            return remote(
                adj_out.at[it] if own else adj_in.at[it, across], adj_in.at[it, mark],
                adj_send.at[it, peer if own else far(peer)], adj_recv.at[it, mark], dict(mem=peer, lat=b),
            )

        def cross_copy(mark):
            return remote(
                adj_out.at[it], adj_in.at[it, mark], adj_send.at[it, across], adj_recv.at[it, mark],
                dict(mem=across, lat=b),
            )

        cross_copy(m).start()

        @pl.loop(0, group - 1)
        def _(i):
            adj_copy(i, 0, True).start()

        adj_in[it, m] = strip_adj
        cross_copy(across).wait()

        @pl.loop(0, group - 1)
        def _(i):
            adj_copy(i, 1, True).start()

        for owner in range(2):

            @pl.loop(0, group - 1)
            def _(i):
                adj_copy(i, owner, False).wait()

        for vl in range(vl_count):
            adj[vl, 0:4] = adj_in[it, 2 * vl]
            adj[vl, 4:8] = adj_in[it, 2 * vl + 1]

        w_from = w_in_last if last else w_in

        def w_copies(k):
            lower, upper = (w_out.at[it, k, 0:16], w_out.at[it, k, 16:32]) if last else (w_out.at[it, k],) * 2
            half = lower.shape[0]
            return [
                remote(
                    lower, w_from.at[k, half : 2 * half], w_send.at[it, 0, k], w_recv.at[it, 1, k],
                    dict(mem=m, lat=south),
                ),
                remote(
                    upper, w_from.at[k, 0:half], w_send.at[it, 1, k], w_recv.at[it, 0, k], dict(mem=m, lat=north)
                ),
            ]

        @pl.loop(0, members)
        def _(k):
            for j in range(lane_tiles):
                lanes = slice(128 * j, 128 * j + 128)
                rows = []
                for level in range(levels):
                    total = jnp.zeros((8, 128), F32)
                    for v in range(variables):
                        vl = v * levels + level
                        total = total + mem[k * vl_count + vl, :, lanes].astype(F32) * adj[vl, :, lanes]
                    rows.append(total)
                if last:
                    rows = [r[0:4] for r in rows] + [r[4:8] for r in rows]
                w_out[it, k, :, lanes] = jnp.concatenate(rows, axis=0).astype(BF16)
            for copy in w_copies(k):
                copy.start()

        def zonal_product(rows, store):
            for at, size in column_chunks(cols):
                part = jnp.dot(rows, z_t[:, at : at + size], preferred_element_type=F32)
                for e in range(size // 128):
                    store(at // 128 + e, part[:, 128 * e : 128 * e + 128])

        def own_rows(j, part):
            for k in range(members):
                for level in range(levels):
                    kl, first = k * levels + level, k * k_rows
                    if last:
                        zp[kl, j, 8:12, :] = part[first + 4 * level : first + 4 * level + 4]
                        first += k_rows // 2
                        zp[kl, j, 12:16, :] = part[first + 4 * level : first + 4 * level + 4]
                    else:
                        zp[kl, j, 8:16, :] = part[first + 8 * level : first + 8 * level + 8]

        zonal_product(w_out[it].reshape(members * k_rows, cols), own_rows)

        coefs = [adjoint_coefs(0)] if last else [adjoint_coefs(-4), adjoint_coefs(4)]

        @pl.loop(0, members)
        def _(k):
            for copy in w_copies(k):
                copy.wait()

            def neighbour_rows(j, part):
                for level in range(levels):
                    kl = k * levels + level
                    if last:
                        zp[kl, j, 4:8, :] = part[4 * level : 4 * level + 4]
                        zp[kl, j, 16:20, :] = part[16 + 4 * level : 20 + 4 * level]
                    else:
                        zp[kl, j, 0:8, :] = part[8 * level : 8 * level + 8]
                        zp[kl, j, 16:24, :] = part[k_rows + 8 * level : k_rows + 8 * level + 8]

            zonal_product(w_from[k], neighbour_rows)

            if last:

                @pl.loop(0, levels)
                def _(level):
                    kl = k * levels + level
                    for j in range(lane_tiles):
                        here = xp[kl, j, 4:12, :]
                        total = jnp.zeros((8, 128), F32)
                        for s in range(2 * HALF + 1):
                            total = total + coefs[0][s] * zp[kl, j, 12 - s : 20 - s, :]
                        out_v[kl, :, 128 * j : 128 * j + 128] = here - STEP * (here + total)

                store(k).start()
            else:
                for part in range(2):

                    @pl.loop(0, levels)
                    def _(level):
                        kl = k * levels + level
                        for j in range(lane_tiles):
                            here = xp[kl, j, 8 * part : 8 * part + 8, :]
                            total = jnp.zeros((8, 128), F32)
                            for s in range(2 * HALF + 1):
                                first = 8 * part + 8 - s
                                total = total + coefs[part][s] * zp[kl, j, first : first + 8, :]
                            xp[kl, j, 8 * part : 8 * part + 8, :] = here - STEP * (here + total)

                spread_rows(k)

    @pl.loop(0, members)
    def _(k):
        store(k).wait()


def body(n_mem, n_lat, members, alpha, zonal_loc, merid_coef, slot_tile, obs_count, obs_index, obs_value, obs_weight):
    k, v, l, rows, cols = members.shape
    slots, n_obs = obs_index.shape[2:]
    kl, vl, lane_tiles = k * l, v * l, cols // 128
    dims = (k, v, l, cols, n_mem, n_lat, slots, n_obs)
    n_taps = merid_coef.shape[1]
    vmem, dma = pltpu.VMEM, pltpu.SemaphoreType.DMA

    def by_slot(array):
        return array.transpose(0, 2, 1, 3).reshape(slots, 1, n_obs)

    out = pl.pallas_call(
        functools.partial(kernel, dims),
        out_shape=jax.ShapeDtypeStruct((kl, rows, cols), F32),
        in_specs=[pl.BlockSpec(memory_space=pl.ANY)] * 7 + [pl.BlockSpec(memory_space=pltpu.SMEM)] * 2,
        out_specs=pl.BlockSpec(memory_space=pl.ANY),
        scratch_shapes=[
            vmem((kl, rows, cols), F32),
            vmem((k * vl, rows, cols), BF16),
            vmem((cols, cols), BF16),
            vmem((cols, cols), BF16),
            vmem((n_taps, n_lat * rows), F32),
            vmem((n_lat * rows + 24, 128), F32),
            vmem((slots, 1, n_obs), jnp.int32),
            vmem((slots, 1, n_obs), F32),
            vmem((slots, 1, n_obs), F32),
            vmem((2, kl, 4, cols), F32),
            vmem((2, kl, 4, cols), F32),
            vmem((kl, lane_tiles, 16, 128), F32),
            vmem((kl * rows, cols), BF16),
            vmem((ITERS, n_mem, 4, cols), F32),
            vmem((ITERS, n_mem, 4, cols), F32),
            vmem((ITERS, 2, 1, cols), F32),
            vmem((ITERS, 2, 1, cols), F32),
            vmem((64 * vl, 128), F32),
            vmem((n_mem, 2 * slots + 1, 8, 128), F32),
            vmem((n_mem, 2 * slots + 1, 8, 128), F32),
            vmem((2 * lane_tiles, 2, 8, 128), F32),
            vmem((4, 16, cols), F32),
            vmem((2, 4, cols), F32),
            vmem((2, 4, cols), F32),
            vmem((ITERS, 4, cols), F32),
            vmem((ITERS, n_mem, 4, cols), F32),
            vmem((vl, 8, cols), F32),
            vmem((ITERS, k, l * rows, cols), BF16),
            vmem((k, 2 * l * rows, cols), BF16),
            vmem((k, l * rows, cols), BF16),
            vmem((kl, lane_tiles, 24, 128), F32),
            vmem((kl, rows, cols), F32),
            dma((7,)), dma((k,)),
            dma((2, k)), dma((2, k)),
            dma((n_mem,)), dma((n_mem,)),
            dma((2,)), dma((2,)),
            dma((ITERS, n_mem)), dma((ITERS, n_mem)),
            dma((ITERS, 2)), dma((ITERS, 2)),
            dma((ITERS, n_mem)), dma((ITERS, n_mem)),
            dma((ITERS, 2, k)), dma((ITERS, 2, k)),
        ],
        compiler_params=pltpu.CompilerParams(
            collective_id=0, has_side_effects=True, vmem_limit_bytes=60 * 1024 * 1024
        ),
    )(
        alpha.reshape(kl, rows, cols),
        members.reshape(k * vl, rows, cols),
        zonal_loc,
        merid_coef.T,
        by_slot(obs_index),
        by_slot(obs_value),
        by_slot(obs_weight),
        slot_tile.reshape(slots),
        obs_count.reshape(slots),
    )
    return out.reshape(alpha.shape)


def solution(mesh):
    in_specs = (
        P("mem", None, None, "lat", None),
        P("mem", None, "lat", None),
        P(),
        P(),
        P("lat", "mem", None),
        P("lat", "mem", None),
        P("lat", "mem", None, None),
        P("lat", "mem", None, None),
        P("lat", "mem", None, None),
    )
    step = functools.partial(body, mesh.shape["mem"], mesh.shape["lat"])
    return jax.shard_map(step, mesh=mesh, in_specs=in_specs, out_specs=P("mem", None, "lat", None), check_vma=False)
```
